256 devices in a mesh: box: 32 (over y_hi, z, core), dir: 8 (over y_lo, x).
Axes of the slice: x: 4, y: 4 (y_hi: 2, y_lo: 2; y = y_hi * 2 + y_lo), z: 8, core: 2. Of those that a mesh axis runs over, the one named last changes fastest.
Arguments:
- leaf_density: bfloat16 [2048, 96, 8, 128], P('box', 'dir'), may hold values from -6 to 6
- phases_first: float32 [8, 96, 64], P(None, 'dir'), may hold values from -3.140625 to 3.140625
- phases_switch: float32 [8, 384, 64], P(None, 'dir'), may hold values from -3.140625 to 3.140625
- phases_top: float32 [8, 1536, 64], P(None, ('box', 'dir')), may hold values from -3.140625 to 3.140625
- transfer_first: bfloat16 [96, 2, 64, 512], P('dir'), may hold values from -0.1875 to 0.1875
- transfer_switch: bfloat16 [384, 2, 64, 512], P('dir'), may hold values from -0.1875 to 0.1875
- transfer_top: bfloat16 [1536, 2, 64, 512], P(('box', 'dir')), may hold values from -0.1875 to 0.1875
- child_mid: int32 [384], P('dir'), may hold values from 0 to 95, as said below
- child_top: int32 [1536], replicated, may hold values from 0 to 383, as said below
Outputs:
- top_density: float32 [4, 1536, 8, 128], P(None, ('box', 'dir'))
The draws below stay inside these ranges and needn't reach their ends.
Inputs may be any that keep to these rules, and one draw needn't show every extreme that they name: `child_mid`: each level-1 wedge contains exactly 4 level-2 wedges. Each level-2 wedge contains exactly 4 level-3 wedges; with j = (w // 6) mod 8, child_top[w] lies in the level-2 wedges j * 48 to (j + 1) * 48 - 1.
All inputs are finite; a program needn't handle non-finite values.
Results may differ from the reference program's by a relative error of at most 0.0064.
Values may be sent and summed in bfloat16 or wider, within the bound.
No kernel may reach another device: no remote copies, remote signals or barrier semaphores. Data moves between devices by JAX's collectives and lax.ppermute only.
A program may use at most 64 MiB of HBM per device.

```python
import jax
import jax.numpy as jnp
from jax import lax

RANK = 64
DIRS_LOW = 96
DIRS_MID = 384
DIRS_TOP = 1536
EXCITATIONS = 8
LEAF_DEV = 64
LEAVES = 2048
N_BOX = 32
N_DIR = 8


def draw_child_mid(key, part):
    shuffled = jax.random.permutation(key, DIRS_MID)
    return (shuffled // 4).astype(jnp.int32)


def draw_child_top(key, part):
    region_size = DIRS_MID // N_DIR
    per_device = DIRS_TOP // (N_BOX * N_DIR)

    def region(region_index):
        shuffled = jax.random.permutation(jax.random.fold_in(key, region_index), 4 * region_size)
        return shuffled // 4 + region_size * region_index
    wedge_table = jax.vmap(region)(jnp.arange(N_DIR))
    wedge_table = wedge_table.reshape(N_DIR, N_BOX, per_device).transpose(1, 0, 2)
    return wedge_table.reshape(DIRS_TOP).astype(jnp.int32)


def block_scale(own_key, shape, shards, least, high):
    def one(dim, shards_of):
        heights = jax.random.uniform(jax.random.fold_in(jax.random.fold_in(own_key, 6), dim), (shards_of,), jnp.float32, least / len(shards), high / len(shards))
        return jnp.repeat(jnp.exp(heights), shape[dim] // shards_of).reshape((-1,) + (1,) * (len(shape) - dim - 1))

    loudness = one(*shards[0])
    for cut in shards[1:]:
        loudness = loudness * one(*cut)
    return loudness


def noise(rng, shape, spread, bound, shards=(), held_as=jnp.bfloat16):
    factor_of = block_scale(rng, shape, shards, -0.22, 0.18) if shards else 1.0
    drawn = jax.random.normal(rng, shape, jnp.float32) * spread * factor_of
    return jnp.minimum(jnp.maximum(drawn, -bound), bound).astype(held_as)


def setup_inputs(seed: int = 0) -> dict:
    splits = jax.random.split(jax.random.key(seed), 10)
    leaf_density = noise(splits[0], (LEAVES, DIRS_LOW, EXCITATIONS, 2 * RANK), 1.0, 6.0, ((0, 32), (1, 8)))
    phases_first = jnp.clip(jax.random.uniform(splits[1], (8, DIRS_LOW, RANK), jnp.float32, -3.140625, 3.140625), -3.140625, 3.140625)
    phases_switch = jnp.clip(jax.random.uniform(splits[2], (8, DIRS_MID, RANK), jnp.float32, -3.140625, 3.140625), -3.140625, 3.140625)
    phases_top = jnp.clip(jax.random.uniform(splits[3], (8, DIRS_TOP, RANK), jnp.float32, -3.140625, 3.140625), -3.140625, 3.140625)
    transfer_first = noise(splits[4], (DIRS_LOW, 2, RANK, 8 * RANK), (16 * RANK) ** -0.5, 0.1875, ((0, 8),))
    transfer_switch = noise(splits[5], (DIRS_MID, 2, RANK, 8 * RANK), (16 * RANK) ** -0.5, 0.1875, ((0, 8),))
    transfer_top = noise(splits[6], (DIRS_TOP, 2, RANK, 8 * RANK), (16 * RANK) ** -0.5, 0.1875, ((0, 256),))
    child_mid = draw_child_mid(jax.random.fold_in(splits[9], 71), 0)
    child_top = draw_child_top(jax.random.fold_in(splits[9], 71), 0)
    return {"leaf_density": leaf_density, "phases_first": phases_first, "phases_switch": phases_switch, "phases_top": phases_top, "transfer_first": transfer_first, "transfer_switch": transfer_switch, "transfer_top": transfer_top, "child_mid": child_mid, "child_top": child_top}


def lift_level(density, angles, transfer):
    box_count, wedges, excite, full_width = density.shape
    half_width = full_width // 2
    parents = box_count // 8
    children = density.reshape(parents, 8, wedges, excite, full_width).astype(jnp.float32)
    real_part = children[..., :half_width]
    imag_part = children[..., half_width:]
    cos_part = jnp.cos(angles)[None, :, :, None, :]
    sine_part = jnp.sin(angles)[None, :, :, None, :]
    phased = jnp.stack([cos_part * real_part - sine_part * imag_part, sine_part * real_part + cos_part * imag_part], axis=4).astype(jnp.bfloat16)
    phased = lax.optimization_barrier(phased).astype(jnp.float32)
    blocks = transfer.astype(jnp.float32).reshape(wedges, 2, half_width, 8, half_width)
    product = jnp.einsum("pcwnsr,wtkcr->pwnstk", phased, blocks, precision=lax.Precision.HIGHEST)
    real_out = product[..., 0, 0, :] - product[..., 1, 1, :]
    imag_out = product[..., 1, 0, :] + product[..., 0, 1, :]
    return jnp.concatenate([real_out, imag_out], axis=-1)


def reference(leaf_density, phases_first, phases_switch, phases_top, transfer_first, transfer_switch, transfer_top, child_mid, child_top):
    groups = leaf_density.shape[0] // LEAF_DEV
    subtrees = leaf_density.reshape((groups, LEAF_DEV) + leaf_density.shape[1:])

    def subtree(leaves):
        level_one = lift_level(leaves, phases_first, transfer_first).astype(jnp.bfloat16)
        selected = jnp.take(level_one, child_mid, axis=1)
        return lift_level(selected, phases_switch, transfer_switch).astype(jnp.bfloat16)[0]

    level_two = lax.map(subtree, subtrees)
    top_input = jnp.take(level_two, child_top, axis=1)
    return lift_level(top_input, phases_top, transfer_top)
```

```python
import jax
import jax.numpy as jnp
from jax import lax
from jax.experimental import pallas as pl
from jax.experimental.pallas import tpu as pltpu
from jax.sharding import PartitionSpec as P

HALF = 64
LANES = 128
EXC = 8
FULL = 8 * HALF
STEP_FIRST = 3
STEP_SWITCH = 8
X_RING = 4
Y_PAIR = 2


def sin_cos(angle):
    turns = jnp.floor(angle * 0.6366197723675814 + 0.5)
    rest = angle - turns * 1.5703125
    rest = rest - turns * 4.837512969970703e-4
    rest = rest - turns * 7.549789948768648e-8
    square = rest * rest
    sine = rest + rest * square * (
        -1.6666654611e-1 + square * (8.3321608736e-3 - square * 1.9515295891e-4)
    )
    cosine = 1.0 - 0.5 * square + square * square * (
        4.166664568298827e-2 + square * (-1.388731625493765e-3 + square * 2.443315711809948e-5)
    )
    quarter = turns.astype(jnp.int32) & 3
    swap = (quarter & 1) == 1
    sine_abs = jnp.where(swap, cosine, sine)
    cosine_abs = jnp.where(swap, sine, cosine)
    sine_out = jnp.where(quarter >= 2, -sine_abs, sine_abs)
    cosine_out = jnp.where((quarter == 1) | (quarter == 2), -cosine_abs, cosine_abs)
    return sine_out, cosine_out


def left_lanes():
    return lax.broadcasted_iota(jnp.int32, (EXC, LANES), 1) < HALF


def flip(value):
    return pltpu.roll(value, HALF, 1)


def pair_up(first, second, left):
    real = jnp.where(left, first, flip(second))
    imag = jnp.where(left, flip(first), second)
    return real, imag


def turned(real, imag, cosine, sine):
    return jnp.concatenate(
        [cosine * real - sine * imag, sine * real + cosine * imag], axis=0
    ).astype(jnp.bfloat16)


def product(rows, weights):
    return lax.dot_general(
        rows, weights, (((1,), (1,)), ((), ())), preferred_element_type=jnp.float32
    )


def joined(real_rows, imag_rows, left):
    moved = flip(imag_rows)
    return real_rows + jnp.where(left, -moved, moved)


def first_kernel(leaf, angles, weights, out, rows, trig):
    left = left_lanes()
    for group in range(4):
        angle = jnp.concatenate([angles[:, 2 * group, :], angles[:, 2 * group + 1, :]], axis=1)
        trig[0, :, group * LANES : (group + 1) * LANES], trig[1, :, group * LANES : (group + 1) * LANES] = sin_cos(angle)
    step = pl.program_id(0)
    for local in range(STEP_FIRST):
        wedge = step * STEP_FIRST + local
        sine = trig[0, pl.ds(wedge, 1), :]
        cosine = trig[1, pl.ds(wedge, 1), :]
        for parent in range(8):
            for group in range(4):
                cut = slice(group * LANES, (group + 1) * LANES)
                child = 8 * parent + 2 * group
                real, imag = pair_up(
                    leaf[child, local].astype(jnp.float32),
                    leaf[child + 1, local].astype(jnp.float32),
                    left,
                )
                rows[parent * 16 : parent * 16 + 16, cut] = turned(real, imag, cosine[:, cut], sine[:, cut])
        result = product(rows[...], weights[local])
        pieces = [
            joined(result[16 * p : 16 * p + 8], result[16 * p + 8 : 16 * p + 16], left)
            for p in range(8)
        ]
        for group in range(4):
            real, imag = pair_up(pieces[2 * group], pieces[2 * group + 1], left)
            out[local, :, group * LANES : (group + 1) * LANES] = jnp.concatenate([real, imag], axis=0).astype(jnp.bfloat16)


def first_level(leaf, angles, weights):
    wedges = leaf.shape[1]
    return pl.pallas_call(
        first_kernel,
        out_shape=jax.ShapeDtypeStruct((wedges, 16, FULL), jnp.bfloat16),
        grid=(wedges // STEP_FIRST,),
        in_specs=[
            pl.BlockSpec((64, STEP_FIRST, EXC, LANES), lambda i: (0, i, 0, 0)),
            pl.BlockSpec((wedges, 8, HALF), lambda i: (0, 0, 0)),
            pl.BlockSpec((STEP_FIRST, LANES, FULL), lambda i: (i, 0, 0)),
        ],
        out_specs=pl.BlockSpec((STEP_FIRST, 16, FULL), lambda i: (i, 0, 0)),
        scratch_shapes=[
            pltpu.VMEM((128, FULL), jnp.bfloat16),
            pltpu.VMEM((2, wedges, FULL), jnp.float32),
        ],
        compiler_params=pltpu.CompilerParams(vmem_limit_bytes=16 << 20),
        name="first_level",
    )(leaf, angles, weights)


def switch_kernel(places, child_mid, child_top, *refs):
    blocks = refs[:8]
    angles, weights, out, gathered, trig, level_two, sems = refs[8:]
    step = pl.program_id(0)
    left = left_lanes()
    low = gathered.shape[0] // 8

    def block_copy(k):
        return pltpu.make_async_copy(
            blocks[k], gathered.at[pl.ds(places[k] * low, low)], sems.at[k]
        )

    @pl.when(step == 0)
    def _():
        for k in range(8):
            block_copy(k).start()
        for group in range(4):
            angle = jnp.concatenate([angles[2 * group], angles[2 * group + 1]], axis=1)
            trig[0, :, group * LANES : (group + 1) * LANES], trig[1, :, group * LANES : (group + 1) * LANES] = sin_cos(angle)
        for k in range(8):
            block_copy(k).wait()

    for local in range(STEP_SWITCH):
        wedge = step * STEP_SWITCH + local
        sine = trig[0, pl.ds(wedge, 1), :]
        cosine = trig[1, pl.ds(wedge, 1), :]
        picked = gathered[child_mid[wedge]].astype(jnp.float32)
        result = product(turned(picked[:8], picked[8:], cosine, sine), weights[local])
        level_two[wedge] = joined(result[:8], result[8:], left).astype(jnp.bfloat16)

    @pl.when(step == pl.num_programs(0) - 1)
    def _():
        mid_count = level_two.shape[0]
        share = places[8]
        devices, top_count = out.shape[0], out.shape[1]
        for device in range(devices):
            for slot in range(top_count):
                top = (device * 8 + share) * top_count + slot
                out[device, slot] = level_two[child_top[top] - share * mid_count]


def switch_level(places, child_mid, child_top, blocks, angles, weights, devices):
    mid_count = weights.shape[0]
    low = blocks[0].shape[0]
    top_count = child_top.shape[0] // (8 * devices)
    return pl.pallas_call(
        switch_kernel,
        out_shape=jax.ShapeDtypeStruct((devices, top_count, EXC, LANES), jnp.bfloat16),
        grid_spec=pltpu.PrefetchScalarGridSpec(
            num_scalar_prefetch=3,
            grid=(mid_count // STEP_SWITCH,),
            in_specs=[pl.BlockSpec(memory_space=pl.ANY)] * 8
            + [
                pl.BlockSpec((8, mid_count, HALF), lambda i, *_: (0, 0, 0)),
                pl.BlockSpec((STEP_SWITCH, LANES, FULL), lambda i, *_: (i, 0, 0)),
            ],
            out_specs=pl.BlockSpec((devices, top_count, EXC, LANES), lambda i, *_: (0, 0, 0, 0)),
            scratch_shapes=[
                pltpu.VMEM((8 * low, 16, FULL), jnp.bfloat16),
                pltpu.VMEM((2, mid_count, FULL), jnp.float32),
                pltpu.VMEM((mid_count, EXC, LANES), jnp.bfloat16),
                pltpu.SemaphoreType.DMA((8,)),
            ],
        ),
        compiler_params=pltpu.CompilerParams(vmem_limit_bytes=24 << 20),
        name="switch_level",
    )(places, child_mid, child_top, *blocks, angles, weights)


def top_kernel(boxes, angles, weights, out, rows, trig):
    left = left_lanes()
    wedges = weights.shape[0]
    for group in range(4):
        angle = jnp.concatenate([angles[:, 2 * group, :], angles[:, 2 * group + 1, :]], axis=1)
        trig[0, :, group * LANES : (group + 1) * LANES], trig[1, :, group * LANES : (group + 1) * LANES] = sin_cos(angle)
    for wedge in range(wedges):
        sine = trig[0, pl.ds(wedge, 1), :]
        cosine = trig[1, pl.ds(wedge, 1), :]
        for parent in range(4):
            for group in range(4):
                cut = slice(group * LANES, (group + 1) * LANES)
                child = 8 * parent + 2 * group
                real, imag = pair_up(
                    boxes[child, wedge].astype(jnp.float32),
                    boxes[child + 1, wedge].astype(jnp.float32),
                    left,
                )
                rows[wedge, parent * 16 : parent * 16 + 16, cut] = turned(real, imag, cosine[:, cut], sine[:, cut])
        result = product(rows[wedge], weights[wedge])
        for p in range(4):
            out[p, wedge] = joined(result[16 * p : 16 * p + 8], result[16 * p + 8 : 16 * p + 16], left)


def top_level(boxes, angles, weights):
    wedges = weights.shape[0]
    return pl.pallas_call(
        top_kernel,
        out_shape=jax.ShapeDtypeStruct((4, wedges, EXC, LANES), jnp.float32),
        scratch_shapes=[
            pltpu.VMEM((wedges, 64, FULL), jnp.bfloat16),
            pltpu.VMEM((2, wedges, FULL), jnp.float32),
        ],
        compiler_params=pltpu.CompilerParams(vmem_limit_bytes=16 << 20),
        name="top_level",
    )(boxes, angles, weights)


def shards(
    leaf_density,
    phases_first,
    phases_switch,
    phases_top,
    transfer_first,
    transfer_switch,
    transfer_top,
    child_mid,
    child_top,
):
    def flat(weights):
        return weights.reshape(weights.shape[0], LANES, FULL)

    level_one = first_level(leaf_density, phases_first.transpose(1, 0, 2), flat(transfer_first))
    here = lax.axis_index("dir").astype(jnp.int32)
    row, column = here // X_RING, here % X_RING
    blocks, places = [], []
    for up in range(Y_PAIR):
        for right in range(X_RING):
            moves = [
                (y * X_RING + x, (y + up) % Y_PAIR * X_RING + (x + right) % X_RING)
                for y in range(Y_PAIR)
                for x in range(X_RING)
            ]
            blocks.append(level_one if up == right == 0 else lax.ppermute(level_one, "dir", moves))
            places.append((row - up) % Y_PAIR * X_RING + (column - right) % X_RING)
    places = jnp.stack(places + [here])
    send = switch_level(
        places, child_mid, child_top, blocks, phases_switch, flat(transfer_switch), lax.axis_size("box")
    )
    boxes = lax.all_to_all(send, "box", 0, 0)
    return top_level(boxes, phases_top.transpose(1, 0, 2), flat(transfer_top))


def solution(mesh):
    placed = (
        P("box", "dir", None, None),
        P(None, "dir", None),
        P(None, "dir", None),
        P(None, ("box", "dir"), None),
        P("dir", None, None, None),
        P("dir", None, None, None),
        P(("box", "dir"), None, None, None),
        P("dir"),
        P(),
    )
    return jax.shard_map(
        shards,
        mesh=mesh,
        in_specs=placed,
        out_specs=P(None, ("box", "dir"), None, None),
        check_vma=False,
    )
```

```python
import jax
import jax.numpy as jnp
from jax import lax
from jax.experimental import pallas as pl
from jax.experimental.pallas import tpu as pltpu
from jax.sharding import PartitionSpec as P

HALF = 64
LANES = 128
EXC = 8
FULL = 8 * HALF
STEP_FIRST = 3
X_RING = 4
Y_PAIR = 2


def sin_cos(angle):
    turns = jnp.floor(angle * 0.6366197723675814 + 0.5)
    rest = angle - turns * 1.5703125
    rest = rest - turns * 4.837512969970703e-4
    rest = rest - turns * 7.549789948768648e-8
    square = rest * rest
    sine = rest + rest * square * (
        -1.6666654611e-1 + square * (8.3321608736e-3 - square * 1.9515295891e-4)
    )
    cosine = 1.0 - 0.5 * square + square * square * (
        4.166664568298827e-2 + square * (-1.388731625493765e-3 + square * 2.443315711809948e-5)
    )
    quarter = turns.astype(jnp.int32) & 3
    swap = (quarter & 1) == 1
    sine_abs = jnp.where(swap, cosine, sine)
    cosine_abs = jnp.where(swap, sine, cosine)
    sine_out = jnp.where(quarter >= 2, -sine_abs, sine_abs)
    cosine_out = jnp.where((quarter == 1) | (quarter == 2), -cosine_abs, cosine_abs)
    return sine_out, cosine_out


def left_lanes():
    return lax.broadcasted_iota(jnp.int32, (EXC, LANES), 1) < HALF


def flip(value):
    return pltpu.roll(value, HALF, 1)


def pair_up(first, second, left):
    real = jnp.where(left, first, flip(second))
    imag = jnp.where(left, flip(first), second)
    return real, imag


def turned(real, imag, cosine, sine):
    return jnp.concatenate(
        [cosine * real - sine * imag, sine * real + cosine * imag], axis=0
    ).astype(jnp.bfloat16)


def product(rows, weights):
    return lax.dot_general(
        rows, weights, (((1,), (1,)), ((), ())), preferred_element_type=jnp.float32
    )


def joined(real_rows, imag_rows, left):
    moved = flip(imag_rows)
    return real_rows + jnp.where(left, -moved, moved)


def in_hbm(value):
    return pltpu.with_memory_space_constraint(value, pltpu.HBM)


def fill_trig(trig, angle_of):
    for group in range(4):
        cut = slice(group * LANES, (group + 1) * LANES)
        angle = jnp.concatenate([angle_of(2 * group), angle_of(2 * group + 1)], axis=1)
        trig[0, :, cut], trig[1, :, cut] = sin_cos(angle)


def first_kernel(leaf_hbm, angles_hbm, weights_hbm, out, leaf, angles, weights, rows, trig, sems):
    left = left_lanes()
    wedges = leaf.shape[1]
    steps = wedges // STEP_FIRST

    def copies(step):
        part = pl.ds(step * STEP_FIRST, STEP_FIRST)
        return (
            pltpu.make_async_copy(leaf_hbm.at[:, part], leaf.at[:, part], sems.at[0, step]),
            pltpu.make_async_copy(weights_hbm.at[part], weights.at[part], sems.at[1, step]),
        )

    angle_copy = pltpu.make_async_copy(angles_hbm, angles, sems.at[0, steps])
    angle_copy.start()
    for step in range(steps):
        for copy in copies(step):
            copy.start()
    angle_copy.wait()
    fill_trig(trig, lambda child: angles[:, child, :])
    for wedge in range(wedges):
        if wedge % STEP_FIRST == 0:
            for copy in copies(wedge // STEP_FIRST):
                copy.wait()
        sine = trig[0, wedge : wedge + 1, :]
        cosine = trig[1, wedge : wedge + 1, :]
        place = wedge % 2
        for parent in range(8):
            for group in range(4):
                cut = slice(group * LANES, (group + 1) * LANES)
                child = 8 * parent + 2 * group
                real, imag = pair_up(
                    leaf[child, wedge].astype(jnp.float32),
                    leaf[child + 1, wedge].astype(jnp.float32),
                    left,
                )
                rows[place, parent * 16 : parent * 16 + 16, cut] = turned(real, imag, cosine[:, cut], sine[:, cut])
        result = product(rows[place], weights[wedge])
        pieces = [
            joined(result[16 * p : 16 * p + 8], result[16 * p + 8 : 16 * p + 16], left)
            for p in range(8)
        ]
        for group in range(4):
            real, imag = pair_up(pieces[2 * group], pieces[2 * group + 1], left)
            out[wedge, :, group * LANES : (group + 1) * LANES] = jnp.concatenate([real, imag], axis=0).astype(jnp.bfloat16)


def first_level(leaf, angles, weights):
    wedges = leaf.shape[1]
    hbm = pl.BlockSpec(memory_space=pltpu.HBM)
    return pl.pallas_call(
        first_kernel,
        out_shape=jax.ShapeDtypeStruct((wedges, 16, FULL), jnp.bfloat16),
        in_specs=[hbm, hbm, hbm],
        scratch_shapes=[
            pltpu.VMEM(leaf.shape, jnp.bfloat16),
            pltpu.VMEM(angles.shape, jnp.float32),
            pltpu.VMEM(weights.shape, jnp.bfloat16),
            pltpu.VMEM((2, 128, FULL), jnp.bfloat16),
            pltpu.VMEM((2, wedges, FULL), jnp.float32),
            pltpu.SemaphoreType.DMA((2, wedges // STEP_FIRST + 1)),
        ],
        compiler_params=pltpu.CompilerParams(vmem_limit_bytes=12 << 20),
        name="first_level",
    )(in_hbm(leaf), in_hbm(angles), in_hbm(weights))


def ready_kernel(angles_hbm, weights_hbm, after, trig, weights, angles, sems):
    weight_copy = pltpu.make_async_copy(weights_hbm, weights, sems.at[0])
    angle_copy = pltpu.make_async_copy(angles_hbm, angles, sems.at[1])
    weight_copy.start()
    angle_copy.start()
    angle_copy.wait()
    fill_trig(trig, lambda child: angles[child])
    weight_copy.wait()


def switch_ready(angles, weights, after):
    hbm = pl.BlockSpec(memory_space=pltpu.HBM)
    return pl.pallas_call(
        ready_kernel,
        out_shape=(
            pltpu.VMEM((2, weights.shape[0], FULL), jnp.float32),
            pltpu.VMEM(weights.shape, jnp.bfloat16),
        ),
        in_specs=[hbm, hbm, pl.BlockSpec(memory_space=pl.ANY)],
        out_specs=(pl.BlockSpec(memory_space=pltpu.VMEM), pl.BlockSpec(memory_space=pltpu.VMEM)),
        scratch_shapes=[pltpu.VMEM(angles.shape, jnp.float32), pltpu.SemaphoreType.DMA((2,))],
        compiler_params=pltpu.CompilerParams(vmem_limit_bytes=4 << 20),
        name="switch_ready",
    )(in_hbm(angles), in_hbm(weights), after)


def switch_kernel(places, child_mid, child_top, *refs):
    blocks = refs[:8]
    trig, weights, out, gathered, level_two, sems = refs[8:]
    left = left_lanes()
    low = gathered.shape[0] // 8
    mid_count = level_two.shape[0]

    def block_copy(k):
        return pltpu.make_async_copy(
            blocks[k], gathered.at[pl.ds(places[k] * low, low)], sems.at[k]
        )

    for k in range(8):
        block_copy(k).start()
    for k in range(8):
        block_copy(k).wait()

    for wedge in range(mid_count):
        sine = trig[0, wedge : wedge + 1, :]
        cosine = trig[1, wedge : wedge + 1, :]
        picked = gathered[child_mid[wedge]].astype(jnp.float32)
        result = product(turned(picked[:8], picked[8:], cosine, sine), weights[wedge])
        level_two[wedge] = joined(result[:8], result[8:], left).astype(jnp.bfloat16)

    share = places[8]
    devices, top_count = out.shape[0], out.shape[1]
    for device in range(devices):
        for slot in range(top_count):
            top = (device * 8 + share) * top_count + slot
            out[device, slot] = level_two[child_top[top] - share * mid_count]


def switch_level(places, child_mid, child_top, blocks, trig, weights, devices):
    mid_count = weights.shape[0]
    low = blocks[0].shape[0]
    top_count = child_top.shape[0] // (8 * devices)
    return pl.pallas_call(
        switch_kernel,
        out_shape=jax.ShapeDtypeStruct((devices, top_count, EXC, LANES), jnp.bfloat16),
        in_specs=[pl.BlockSpec(memory_space=pltpu.SMEM)] * 3
        + [pl.BlockSpec(memory_space=pl.ANY)] * 8
        + [pl.BlockSpec(memory_space=pltpu.VMEM)] * 2,
        scratch_shapes=[
            pltpu.VMEM((8 * low, 16, FULL), jnp.bfloat16),
            pltpu.VMEM((mid_count, EXC, LANES), jnp.bfloat16),
            pltpu.SemaphoreType.DMA((8,)),
        ],
        compiler_params=pltpu.CompilerParams(vmem_limit_bytes=12 << 20),
        name="switch_level",
    )(places, child_mid, child_top, *blocks, trig, weights)


def top_kernel(boxes, angles, weights, out, rows, trig):
    left = left_lanes()
    wedges = weights.shape[0]
    for group in range(4):
        angle = jnp.concatenate([angles[:, 2 * group, :], angles[:, 2 * group + 1, :]], axis=1)
        trig[0, :, group * LANES : (group + 1) * LANES], trig[1, :, group * LANES : (group + 1) * LANES] = sin_cos(angle)
    for wedge in range(wedges):
        sine = trig[0, pl.ds(wedge, 1), :]
        cosine = trig[1, pl.ds(wedge, 1), :]
        for parent in range(4):
            for group in range(4):
                cut = slice(group * LANES, (group + 1) * LANES)
                child = 8 * parent + 2 * group
                real, imag = pair_up(
                    boxes[child, wedge].astype(jnp.float32),
                    boxes[child + 1, wedge].astype(jnp.float32),
                    left,
                )
                rows[wedge, parent * 16 : parent * 16 + 16, cut] = turned(real, imag, cosine[:, cut], sine[:, cut])
        result = product(rows[wedge], weights[wedge])
        for p in range(4):
            out[p, wedge] = joined(result[16 * p : 16 * p + 8], result[16 * p + 8 : 16 * p + 16], left)


def top_level(boxes, angles, weights):
    wedges = weights.shape[0]
    return pl.pallas_call(
        top_kernel,
        out_shape=jax.ShapeDtypeStruct((4, wedges, EXC, LANES), jnp.float32),
        scratch_shapes=[
            pltpu.VMEM((wedges, 64, FULL), jnp.bfloat16),
            pltpu.VMEM((2, wedges, FULL), jnp.float32),
        ],
        compiler_params=pltpu.CompilerParams(vmem_limit_bytes=16 << 20),
        name="top_level",
    )(boxes, angles, weights)


def shards(
    leaf_density,
    phases_first,
    phases_switch,
    phases_top,
    transfer_first,
    transfer_switch,
    transfer_top,
    child_mid,
    child_top,
):
    def flat(weights):
        return weights.reshape(weights.shape[0], LANES, FULL)

    level_one = first_level(leaf_density, phases_first.transpose(1, 0, 2), flat(transfer_first))
    here = lax.axis_index("dir").astype(jnp.int32)
    box = lax.axis_index("box").astype(jnp.int32)
    boxes = lax.axis_size("box")

    def moves(up, right):
        pairs = []
        for b in range(boxes):
            for y in range(Y_PAIR):
                for x in range(X_RING):
                    side = right if b % 2 == 0 else -right
                    to_y, to_x = (y + up) % Y_PAIR, (x + side) % X_RING
                    pairs.append(((b * Y_PAIR + y) * X_RING + x, (b * Y_PAIR + to_y) * X_RING + to_x))
        return pairs

    def shift(block, up, right):
        return lax.ppermute(block, ("box", "dir"), moves(up, right))

    other = shift(level_one, 1, 0)
    front = shift(level_one, 0, 1)
    back = shift(level_one, 0, -1)
    far = shift(front, 0, 1)
    other_front = shift(other, 0, 1)
    other_back = shift(back, 1, 0)
    other_far = shift(other_front, 0, 1)
    blocks = (level_one, other, front, back, far, other_front, other_back, other_far)
    offsets = ((0, 0), (1, 0), (0, 1), (0, -1), (0, 2), (1, 1), (1, -1), (1, 2))
    table = [
        [
            (y + up) % Y_PAIR * X_RING + (x - right * side) % X_RING
            for up, right in offsets
        ]
        + [y * X_RING + x]
        for side in (1, -1)
        for y in range(Y_PAIR)
        for x in range(X_RING)
    ]
    places = jnp.asarray(table, jnp.int32)[box % 2 * Y_PAIR * X_RING + here]
    trig, weights = switch_ready(phases_switch, flat(transfer_switch), front)
    send = switch_level(places, child_mid, child_top, blocks, trig, weights, boxes)
    received = lax.all_to_all(send, "box", 0, 0)
    return top_level(received, phases_top.transpose(1, 0, 2), flat(transfer_top))


def solution(mesh):
    placed = (
        P("box", "dir", None, None),
        P(None, "dir", None),
        P(None, "dir", None),
        P(None, ("box", "dir"), None),
        P("dir", None, None, None),
        P("dir", None, None, None),
        P(("box", "dir"), None, None, None),
        P("dir"),
        P(),
    )
    return jax.shard_map(
        shards,
        mesh=mesh,
        in_specs=placed,
        out_specs=P(None, ("box", "dir"), None, None),
        check_vma=False,
    )
```

```python
import functools

import jax
import jax.numpy as jnp
from jax import lax
from jax.experimental import pallas as pl
from jax.experimental.pallas import tpu as pltpu
from jax.sharding import PartitionSpec as P


HALF = 64
LANES = 128
EXC = 8
FULL = 8 * HALF
STEP_FIRST = 3
BATCH = 8
X_RING = 4
Y_PAIR = 2
OFFSETS = ((0, 0), (1, 0), (0, 1), (0, -1), (0, 2), (1, 1), (1, -1), (1, 2))


def sin_cos(angle):
    turns = jnp.floor(angle * 0.6366197723675814 + 0.5)
    rest = angle - turns * 1.5703125
    rest = rest - turns * 4.837512969970703e-4
    rest = rest - turns * 7.549789948768648e-8
    square = rest * rest
    sine = rest + rest * square * (
        -1.6666654611e-1 + square * (8.3321608736e-3 - square * 1.9515295891e-4)
    )
    cosine = 1.0 - 0.5 * square + square * square * (
        4.166664568298827e-2 + square * (-1.388731625493765e-3 + square * 2.443315711809948e-5)
    )
    quarter = turns.astype(jnp.int32) & 3
    swap = (quarter & 1) == 1
    sine_abs = jnp.where(swap, cosine, sine)
    cosine_abs = jnp.where(swap, sine, cosine)
    sine_out = jnp.where(quarter >= 2, -sine_abs, sine_abs)
    cosine_out = jnp.where((quarter == 1) | (quarter == 2), -cosine_abs, cosine_abs)
    return sine_out, cosine_out


def left_lanes():
    return lax.broadcasted_iota(jnp.int32, (EXC, LANES), 1) < HALF


def flip(value):
    return pltpu.roll(value, HALF, 1)


def pair_up(first, second, left):
    real = jnp.where(left, first, flip(second))
    imag = jnp.where(left, flip(first), second)
    return real, imag


def turned(real, imag, cosine, sine):
    return jnp.concatenate(
        [cosine * real - sine * imag, sine * real + cosine * imag], axis=0
    ).astype(jnp.bfloat16)


def product(rows, weights):
    return lax.dot_general(
        rows, weights, (((1,), (1,)), ((), ())), preferred_element_type=jnp.float32
    )


def joined(real_rows, imag_rows, left):
    moved = flip(imag_rows)
    return real_rows + jnp.where(left, -moved, moved)


def in_hbm(value):
    return pltpu.with_memory_space_constraint(value, pltpu.HBM)


def fill_trig(trig, angle_of):
    for group in range(4):
        cut = slice(group * LANES, (group + 1) * LANES)
        angle = jnp.concatenate([angle_of(2 * group), angle_of(2 * group + 1)], axis=1)
        trig[0, :, cut], trig[1, :, cut] = sin_cos(angle)


def first_kernel(leaf_hbm, angles_hbm, weights_hbm, out, leaf, angles, weights, rows, trig, sems):
    left = left_lanes()
    wedges = leaf.shape[1]
    steps = wedges // STEP_FIRST

    def copies(step):
        part = pl.ds(step * STEP_FIRST, STEP_FIRST)
        return (
            pltpu.make_async_copy(leaf_hbm.at[:, part], leaf.at[:, part], sems.at[0, step]),
            pltpu.make_async_copy(weights_hbm.at[part], weights.at[part], sems.at[1, step]),
        )

    angle_copy = pltpu.make_async_copy(angles_hbm, angles, sems.at[0, steps])
    angle_copy.start()
    for step in range(steps):
        for copy in copies(step):
            copy.start()
    angle_copy.wait()
    fill_trig(trig, lambda child: angles[:, child, :])
    for wedge in range(wedges):
        if wedge % STEP_FIRST == 0:
            for copy in copies(wedge // STEP_FIRST):
                copy.wait()
        sine = trig[0, wedge : wedge + 1, :]
        cosine = trig[1, wedge : wedge + 1, :]
        place = wedge % 2
        for parent in range(8):
            for group in range(4):
                cut = slice(group * LANES, (group + 1) * LANES)
                child = 8 * parent + 2 * group
                real, imag = pair_up(
                    leaf[child, wedge].astype(jnp.float32),
                    leaf[child + 1, wedge].astype(jnp.float32),
                    left,
                )
                rows[place, parent * 16 : parent * 16 + 16, cut] = turned(real, imag, cosine[:, cut], sine[:, cut])
        result = product(rows[place], weights[wedge])
        pieces = [
            joined(result[16 * p : 16 * p + 8], result[16 * p + 8 : 16 * p + 16], left)
            for p in range(8)
        ]
        for group in range(4):
            real, imag = pair_up(pieces[2 * group], pieces[2 * group + 1], left)
            out[wedge, :, group * LANES : (group + 1) * LANES] = jnp.concatenate([real, imag], axis=0).astype(jnp.bfloat16)


def first_level(leaf, angles, weights):
    wedges = leaf.shape[1]
    hbm = pl.BlockSpec(memory_space=pltpu.HBM)
    return pl.pallas_call(
        first_kernel,
        out_shape=jax.ShapeDtypeStruct((wedges, 16, FULL), jnp.bfloat16),
        in_specs=[hbm, hbm, hbm],
        scratch_shapes=[
            pltpu.VMEM(leaf.shape, jnp.bfloat16),
            pltpu.VMEM(angles.shape, jnp.float32),
            pltpu.VMEM(weights.shape, jnp.bfloat16),
            pltpu.VMEM((2, 128, FULL), jnp.bfloat16),
            pltpu.VMEM((2, wedges, FULL), jnp.float32),
            pltpu.SemaphoreType.DMA((2, wedges // STEP_FIRST + 1)),
        ],
        compiler_params=pltpu.CompilerParams(vmem_limit_bytes=12 << 20),
        name="first_level",
    )(in_hbm(leaf), in_hbm(angles), in_hbm(weights))


def ready_kernel(switch_hbm, top_hbm, weights_hbm, after, switch_trig, top_trig, weights, switch_angles, top_angles, sems):
    weight_copy = pltpu.make_async_copy(weights_hbm, weights, sems.at[0])
    switch_copy = pltpu.make_async_copy(switch_hbm, switch_angles, sems.at[1])
    top_copy = pltpu.make_async_copy(top_hbm, top_angles, sems.at[2])
    switch_copy.start()
    top_copy.start()
    weight_copy.start()
    switch_copy.wait()
    fill_trig(switch_trig, lambda child: switch_angles[child])
    top_copy.wait()
    fill_trig(top_trig, lambda child: top_angles[:, child, :])
    weight_copy.wait()


def make_ready(switch_angles, top_angles, weights, after):
    hbm = pl.BlockSpec(memory_space=pltpu.HBM)
    vmem = pl.BlockSpec(memory_space=pltpu.VMEM)
    return pl.pallas_call(
        ready_kernel,
        out_shape=(
            pltpu.VMEM((2, weights.shape[0], FULL), jnp.float32),
            pltpu.VMEM((2, top_angles.shape[0], FULL), jnp.float32),
            pltpu.VMEM(weights.shape, jnp.bfloat16),
        ),
        in_specs=[hbm, hbm, hbm, pl.BlockSpec(memory_space=pl.ANY)],
        out_specs=(vmem, vmem, vmem),
        scratch_shapes=[
            pltpu.VMEM(switch_angles.shape, jnp.float32),
            pltpu.VMEM(top_angles.shape, jnp.float32),
            pltpu.SemaphoreType.DMA((3,)),
        ],
        compiler_params=pltpu.CompilerParams(vmem_limit_bytes=4 << 20),
        name="make_ready",
    )(in_hbm(switch_angles), in_hbm(top_angles), in_hbm(weights), after)


def lift_one(picked, trig, weights, wedge, left):
    rows = picked.astype(jnp.float32)
    sine = trig[0, pl.ds(wedge, 1), :]
    cosine = trig[1, pl.ds(wedge, 1), :]
    result = product(turned(rows[:8], rows[8:], cosine, sine), weights[wedge])
    return joined(result[:8], result[8:], left).astype(jnp.bfloat16)


def most_kernel(top_count, child_mid, child_top, *refs):
    blocks = refs[:7]
    trig, weights, level_two, plan, gathered = refs[7:]
    left = left_lanes()
    low = gathered.shape[0] // 8
    mid_count = level_two.shape[0]
    slots = plan.shape[0] - 4 * mid_count
    share = lax.axis_index("dir").astype(jnp.int32)
    ahead = 1 - 2 * (lax.axis_index("box").astype(jnp.int32) & 1)
    row, column = share >> 2, share & (X_RING - 1)

    def first_wedge(up, right):
        return low * (((row + up) & 1) * X_RING + ((column - right * ahead) & (X_RING - 1)))

    far = first_wedge(*OFFSETS[7])

    for k in range(7):
        base = first_wedge(*OFFSETS[k])
        for i in range(low):
            gathered[base + i] = blocks[k][i]

    for wedge in range(mid_count):
        source = child_mid[wedge]
        is_far = (source >= far) & (source < far + low)
        picked = gathered[jnp.where(is_far, share * low, source)]
        level_two[wedge] = lift_one(picked, trig, weights, wedge, left)

    def note(wedge, count):
        row = child_mid[wedge] - far
        plan[slots + count] = wedge
        plan[slots + mid_count + count] = row
        return count + jnp.where((row >= 0) & (row < low), 1, 0)

    count = lax.fori_loop(0, mid_count, note, jnp.int32(0))
    plan[slots + 2 * mid_count] = count

    def pad(i, carry):
        plan[slots + i] = plan[slots]
        plan[slots + mid_count + i] = plan[slots + mid_count]
        return carry

    lax.fori_loop(count, mid_count, pad, 0)

    def place(device, carry):
        for slot in range(top_count):
            top = (device * 8 + share) * top_count + slot
            plan[device * top_count + slot] = child_top[top] - share * mid_count
        return carry

    lax.fori_loop(0, slots // top_count, place, 0)


def switch_most(child_mid, child_top, blocks, trig, weights, top_count):
    mid_count = weights.shape[0]
    low = blocks[0].shape[0]
    smem = pl.BlockSpec(memory_space=pltpu.SMEM)
    vmem = pl.BlockSpec(memory_space=pltpu.VMEM)
    return pl.pallas_call(
        functools.partial(most_kernel, top_count),
        out_shape=(
            pltpu.VMEM((mid_count, EXC, LANES), jnp.bfloat16),
            jax.ShapeDtypeStruct((child_top.shape[0] // 8 + 4 * mid_count,), jnp.int32),
        ),
        in_specs=[smem] * 2 + [vmem] * 9,
        out_specs=(vmem, smem),
        scratch_shapes=[pltpu.VMEM((8 * low, 16, FULL), jnp.bfloat16)],
        compiler_params=pltpu.CompilerParams(vmem_limit_bytes=8 << 20),
        name="switch_most",
    )(child_mid, child_top, *blocks, trig, weights)


def rest_kernel(plan, block, trig, weights, ready, out, level_two):
    left = left_lanes()
    mid_count = level_two.shape[0]
    slots = plan.shape[0] - 4 * mid_count
    for wedge in range(mid_count):
        level_two[wedge] = ready[wedge]

    def batch(step, carry):
        for i in range(BATCH):
            wedge = plan[slots + step * BATCH + i]
            row = plan[slots + mid_count + step * BATCH + i]
            level_two[wedge] = lift_one(block[row], trig, weights, wedge, left)
        return carry

    lax.fori_loop(0, (plan[slots + 2 * mid_count] + BATCH - 1) // BATCH, batch, 0)
    top_count = out.shape[1]
    for slot in range(slots):
        out[slot // top_count, slot % top_count] = level_two[plan[slot]]


def switch_rest(plan, block, trig, weights, ready, devices):
    mid_count = weights.shape[0]
    slots = plan.shape[0] - 4 * mid_count
    vmem = pl.BlockSpec(memory_space=pltpu.VMEM)
    return pl.pallas_call(
        rest_kernel,
        out_shape=jax.ShapeDtypeStruct((devices, slots // devices, EXC, LANES), jnp.bfloat16),
        in_specs=[pl.BlockSpec(memory_space=pltpu.SMEM)] + [vmem] * 4,
        scratch_shapes=[pltpu.VMEM((mid_count, EXC, LANES), jnp.bfloat16)],
        compiler_params=pltpu.CompilerParams(vmem_limit_bytes=4 << 20),
        name="switch_rest",
    )(plan, block, trig, weights, ready)


def top_kernel(boxes, trig, weights, out, rows):
    left = left_lanes()
    wedges = weights.shape[0]
    for wedge in range(wedges):
        sine = trig[0, pl.ds(wedge, 1), :]
        cosine = trig[1, pl.ds(wedge, 1), :]
        for parent in range(4):
            for group in range(4):
                cut = slice(group * LANES, (group + 1) * LANES)
                child = 8 * parent + 2 * group
                real, imag = pair_up(
                    boxes[child, wedge].astype(jnp.float32),
                    boxes[child + 1, wedge].astype(jnp.float32),
                    left,
                )
                rows[wedge, parent * 16 : parent * 16 + 16, cut] = turned(real, imag, cosine[:, cut], sine[:, cut])
        result = product(rows[wedge], weights[wedge])
        for p in range(4):
            out[p, wedge] = joined(result[16 * p : 16 * p + 8], result[16 * p + 8 : 16 * p + 16], left)


def top_level(boxes, trig, weights):
    wedges = weights.shape[0]
    return pl.pallas_call(
        top_kernel,
        out_shape=jax.ShapeDtypeStruct((4, wedges, EXC, LANES), jnp.float32),
        scratch_shapes=[
            pltpu.VMEM((wedges, 64, FULL), jnp.bfloat16),
        ],
        compiler_params=pltpu.CompilerParams(vmem_limit_bytes=16 << 20),
        name="top_level",
    )(boxes, trig, weights)


def upward(
    leaf_density,
    phases_first,
    phases_switch,
    phases_top,
    transfer_first,
    transfer_switch,
    transfer_top,
    child_mid,
    child_top,
):
    def flat(weights):
        return weights.reshape(weights.shape[0], LANES, FULL)

    level_one = first_level(leaf_density, phases_first.transpose(1, 0, 2), flat(transfer_first))
    boxes = lax.axis_size("box")

    def moves(up, right):
        pairs = []
        for b in range(boxes):
            for y in range(Y_PAIR):
                for x in range(X_RING):
                    side = right if b % 2 == 0 else -right
                    to_y, to_x = (y + up) % Y_PAIR, (x + side) % X_RING
                    pairs.append(((b * Y_PAIR + y) * X_RING + x, (b * Y_PAIR + to_y) * X_RING + to_x))
        return pairs

    def shift(block, up, right):
        return lax.ppermute(block, ("box", "dir"), moves(up, right))

    other = shift(level_one, 1, 0)
    front = shift(level_one, 0, 1)
    back = shift(level_one, 0, -1)
    far = shift(front, 0, 1)
    other_front = shift(other, 0, 1)
    other_back = shift(back, 1, 0)
    other_far = shift(other_front, 0, 1)
    blocks = (level_one, other, front, back, far, other_front, other_back, other_far)
    switch_trig, top_trig, weights = make_ready(
        phases_switch, phases_top.transpose(1, 0, 2), flat(transfer_switch), level_one
    )
    most, plan = switch_most(
        child_mid, child_top, blocks[:7], switch_trig, weights, transfer_top.shape[0]
    )
    send = switch_rest(plan, other_far, switch_trig, weights, most, boxes)
    received = lax.all_to_all(send, "box", 0, 0)
    return top_level(received, top_trig, flat(transfer_top))


def solution(mesh):
    placed = (
        P("box", "dir", None, None),
        P(None, "dir", None),
        P(None, "dir", None),
        P(None, ("box", "dir"), None),
        P("dir", None, None, None),
        P("dir", None, None, None),
        P(("box", "dir"), None, None, None),
        P("dir"),
        P(),
    )
    return jax.shard_map(
        upward,
        mesh=mesh,
        in_specs=placed,
        out_specs=P(None, ("box", "dir"), None, None),
        check_vma=False,
    )
```

```python
import functools

import jax
import jax.numpy as jnp
from jax import lax
from jax.experimental import pallas as pl
from jax.experimental.pallas import tpu as pltpu
from jax.sharding import PartitionSpec as P


HALF = 64
LANES = 128
EXC = 8
FULL = 8 * HALF
STEP_FIRST = 6
BATCH = 8
X_RING = 4
Y_PAIR = 2
OFFSETS = ((0, 0), (1, 0), (0, 1), (0, -1), (0, 2), (1, 1), (1, -1), (1, 2))


def sin_cos(angle):
    turns = jnp.floor(angle * 0.6366197723675814 + 0.5)
    rest = angle - turns * 1.5703125
    rest = rest - turns * 4.837512969970703e-4
    rest = rest - turns * 7.549789948768648e-8
    square = rest * rest
    sine = rest + rest * square * (
        -1.6666654611e-1 + square * (8.3321608736e-3 - square * 1.9515295891e-4)
    )
    cosine = 1.0 - 0.5 * square + square * square * (
        4.166664568298827e-2 + square * (-1.388731625493765e-3 + square * 2.443315711809948e-5)
    )
    quarter = turns.astype(jnp.int32) & 3
    swap = (quarter & 1) == 1
    sine_abs = jnp.where(swap, cosine, sine)
    cosine_abs = jnp.where(swap, sine, cosine)
    sine_out = jnp.where(quarter >= 2, -sine_abs, sine_abs)
    cosine_out = jnp.where((quarter == 1) | (quarter == 2), -cosine_abs, cosine_abs)
    return sine_out, cosine_out


def left_lanes():
    return lax.broadcasted_iota(jnp.int32, (EXC, LANES), 1) < HALF


def flip(value):
    return pltpu.roll(value, HALF, 1)


def pair_up(first, second, left):
    real = jnp.where(left, first, flip(second))
    imag = jnp.where(left, flip(first), second)
    return real, imag


def turned(real, imag, cosine, sine):
    return jnp.concatenate(
        [cosine * real - sine * imag, sine * real + cosine * imag], axis=0
    ).astype(jnp.bfloat16)


def product(rows, weights):
    return lax.dot_general(
        rows, weights, (((1,), (1,)), ((), ())), preferred_element_type=jnp.float32
    )


def joined(real_rows, imag_rows, left):
    moved = flip(imag_rows)
    return real_rows + jnp.where(left, -moved, moved)


def in_hbm(value):
    return pltpu.with_memory_space_constraint(value, pltpu.HBM)


def fill_trig(trig, angle_of):
    for group in range(4):
        cut = slice(group * LANES, (group + 1) * LANES)
        angle = jnp.concatenate([angle_of(2 * group), angle_of(2 * group + 1)], axis=1)
        trig[0, :, cut], trig[1, :, cut] = sin_cos(angle)


def first_kernel(leaf_hbm, angles_hbm, weights_hbm, later_hbm, out, later, leaf, angles, weights, rows, trig, sems):
    left = left_lanes()
    wedges = leaf.shape[1]
    steps = wedges // STEP_FIRST

    def copies(step):
        part = pl.ds(step * STEP_FIRST, STEP_FIRST)
        return (
            pltpu.make_async_copy(leaf_hbm.at[:, part], leaf.at[:, part], sems.at[0, step]),
            pltpu.make_async_copy(weights_hbm.at[part], weights.at[part], sems.at[1, step]),
        )

    angle_copy = pltpu.make_async_copy(angles_hbm, angles, sems.at[0, steps])
    later_copy = pltpu.make_async_copy(later_hbm, later, sems.at[1, steps])
    angle_copy.start()
    for step in range(steps):
        for copy in copies(step):
            copy.start()
    later_copy.start()
    angle_copy.wait()
    fill_trig(trig, lambda child: angles[:, child, :])
    for wedge in range(wedges):
        if wedge % STEP_FIRST == 0:
            for copy in copies(wedge // STEP_FIRST):
                copy.wait()
        sine = trig[0, wedge : wedge + 1, :]
        cosine = trig[1, wedge : wedge + 1, :]
        place = wedge % 2
        for parent in range(8):
            for group in range(4):
                cut = slice(group * LANES, (group + 1) * LANES)
                child = 8 * parent + 2 * group
                real, imag = pair_up(
                    leaf[child, wedge].astype(jnp.float32),
                    leaf[child + 1, wedge].astype(jnp.float32),
                    left,
                )
                rows[place, parent * 16 : parent * 16 + 16, cut] = turned(real, imag, cosine[:, cut], sine[:, cut])
        result = product(rows[place], weights[wedge])
        pieces = [
            joined(result[16 * p : 16 * p + 8], result[16 * p + 8 : 16 * p + 16], left)
            for p in range(8)
        ]
        for group in range(4):
            real, imag = pair_up(pieces[2 * group], pieces[2 * group + 1], left)
            out[wedge, :, group * LANES : (group + 1) * LANES] = jnp.concatenate([real, imag], axis=0).astype(jnp.bfloat16)
    later_copy.wait()


def first_level(leaf, angles, weights, later):
    wedges = leaf.shape[1]
    hbm = pl.BlockSpec(memory_space=pltpu.HBM)
    return pl.pallas_call(
        first_kernel,
        out_shape=(
            pltpu.VMEM((wedges, 16, FULL), jnp.bfloat16),
            pltpu.VMEM(later.shape, jnp.bfloat16),
        ),
        in_specs=[hbm, hbm, hbm, hbm],
        out_specs=(pl.BlockSpec(memory_space=pltpu.VMEM), pl.BlockSpec(memory_space=pltpu.VMEM)),
        scratch_shapes=[
            pltpu.VMEM(leaf.shape, jnp.bfloat16),
            pltpu.VMEM(angles.shape, jnp.float32),
            pltpu.VMEM(weights.shape, jnp.bfloat16),
            pltpu.VMEM((2, 128, FULL), jnp.bfloat16),
            pltpu.VMEM((2, wedges, FULL), jnp.float32),
            pltpu.SemaphoreType.DMA((2, wedges // STEP_FIRST + 1)),
        ],
        compiler_params=pltpu.CompilerParams(vmem_limit_bytes=12 << 20),
        name="first_level",
    )(in_hbm(leaf), in_hbm(angles), in_hbm(weights), in_hbm(later))


def ready_kernel(switch_hbm, top_hbm, after, switch_trig, top_trig, switch_angles, top_angles, sems):
    switch_copy = pltpu.make_async_copy(switch_hbm, switch_angles, sems.at[0])
    top_copy = pltpu.make_async_copy(top_hbm, top_angles, sems.at[1])
    switch_copy.start()
    top_copy.start()
    switch_copy.wait()
    fill_trig(switch_trig, lambda child: switch_angles[child])
    top_copy.wait()
    fill_trig(top_trig, lambda child: top_angles[:, child, :])


def make_ready(switch_angles, top_angles, after):
    hbm = pl.BlockSpec(memory_space=pltpu.HBM)
    vmem = pl.BlockSpec(memory_space=pltpu.VMEM)
    return pl.pallas_call(
        ready_kernel,
        out_shape=(
            pltpu.VMEM((2, switch_angles.shape[1], FULL), jnp.float32),
            pltpu.VMEM((2, top_angles.shape[0], FULL), jnp.float32),
        ),
        in_specs=[hbm, hbm, pl.BlockSpec(memory_space=pl.ANY)],
        out_specs=(vmem, vmem),
        scratch_shapes=[
            pltpu.VMEM(switch_angles.shape, jnp.float32),
            pltpu.VMEM(top_angles.shape, jnp.float32),
            pltpu.SemaphoreType.DMA((2,)),
        ],
        compiler_params=pltpu.CompilerParams(vmem_limit_bytes=4 << 20),
        name="make_ready",
    )(in_hbm(switch_angles), in_hbm(top_angles), after)


def lift_one(picked, trig, weights, wedge, left):
    rows = picked.astype(jnp.float32)
    sine = trig[0, pl.ds(wedge, 1), :]
    cosine = trig[1, pl.ds(wedge, 1), :]
    result = product(turned(rows[:8], rows[8:], cosine, sine), weights[wedge])
    return joined(result[:8], result[8:], left).astype(jnp.bfloat16)


def most_kernel(top_count, child_mid, child_top, *refs):
    blocks = refs[:7]
    trig, weights, level_two, plan, gathered = refs[7:]
    left = left_lanes()
    low = gathered.shape[0] // 8
    mid_count = level_two.shape[0]
    slots = plan.shape[0] - 4 * mid_count
    share = lax.axis_index("dir").astype(jnp.int32)
    ahead = 1 - 2 * (lax.axis_index("box").astype(jnp.int32) & 1)
    row, column = share >> 2, share & (X_RING - 1)

    def first_wedge(up, right):
        return low * (((row + up) & 1) * X_RING + ((column - right * ahead) & (X_RING - 1)))

    far = first_wedge(*OFFSETS[7])

    for k in range(7):
        base = first_wedge(*OFFSETS[k])
        for i in range(low):
            gathered[base + i] = blocks[k][i]

    count = jnp.int32(0)
    per_wedge = slots // mid_count
    for wedge in range(mid_count):
        source = child_mid[wedge]
        row = source - far
        is_far = (row >= 0) & (row < low)
        plan[slots + count] = wedge
        plan[slots + mid_count + count] = row
        count = count + jnp.where(is_far, 1, 0)
        picked = gathered[jnp.where(is_far, share * low, source)]
        level_two[wedge] = lift_one(picked, trig, weights, wedge, left)
        for slot in range(per_wedge * wedge, per_wedge * (wedge + 1)):
            top = (slot // top_count * 8 + share) * top_count + slot % top_count
            plan[slot] = child_top[top] - share * mid_count
    plan[slots + 2 * mid_count] = count


def switch_most(child_mid, child_top, blocks, trig, weights, top_count):
    mid_count = weights.shape[0]
    low = blocks[0].shape[0]
    smem = pl.BlockSpec(memory_space=pltpu.SMEM)
    vmem = pl.BlockSpec(memory_space=pltpu.VMEM)
    return pl.pallas_call(
        functools.partial(most_kernel, top_count),
        out_shape=(
            pltpu.VMEM((mid_count, EXC, LANES), jnp.bfloat16),
            jax.ShapeDtypeStruct((child_top.shape[0] // 8 + 4 * mid_count,), jnp.int32),
        ),
        in_specs=[smem] * 2 + [vmem] * 9,
        out_specs=(vmem, smem),
        scratch_shapes=[pltpu.VMEM((8 * low, 16, FULL), jnp.bfloat16)],
        compiler_params=pltpu.CompilerParams(vmem_limit_bytes=8 << 20),
        name="switch_most",
    )(child_mid, child_top, *blocks, trig, weights)


def rest_kernel(plan, block, trig, weights, ready, out, level_two):
    left = left_lanes()
    mid_count = level_two.shape[0]
    slots = plan.shape[0] - 4 * mid_count
    for wedge in range(mid_count):
        level_two[wedge] = ready[wedge]

    count = plan[slots + 2 * mid_count]

    def batch(step, carry):
        for i in range(BATCH):
            entry = slots + jnp.minimum(step * BATCH + i, count - 1)
            wedge = plan[entry]
            row = plan[mid_count + entry]
            level_two[wedge] = lift_one(block[row], trig, weights, wedge, left)
        return carry

    lax.fori_loop(0, (count + BATCH - 1) // BATCH, batch, 0)
    top_count = out.shape[1]
    for slot in range(slots):
        out[slot // top_count, slot % top_count] = level_two[plan[slot]]


def switch_rest(plan, block, trig, weights, ready, devices):
    mid_count = weights.shape[0]
    slots = plan.shape[0] - 4 * mid_count
    vmem = pl.BlockSpec(memory_space=pltpu.VMEM)
    return pl.pallas_call(
        rest_kernel,
        out_shape=jax.ShapeDtypeStruct((devices, slots // devices, EXC, LANES), jnp.bfloat16),
        in_specs=[pl.BlockSpec(memory_space=pltpu.SMEM)] + [vmem] * 4,
        scratch_shapes=[pltpu.VMEM((mid_count, EXC, LANES), jnp.bfloat16)],
        compiler_params=pltpu.CompilerParams(vmem_limit_bytes=4 << 20),
        name="switch_rest",
    )(plan, block, trig, weights, ready)


def top_kernel(boxes, trig, weights, out, rows):
    left = left_lanes()
    wedges = weights.shape[0]
    for wedge in range(wedges):
        sine = trig[0, pl.ds(wedge, 1), :]
        cosine = trig[1, pl.ds(wedge, 1), :]
        for parent in range(4):
            for group in range(4):
                cut = slice(group * LANES, (group + 1) * LANES)
                child = 8 * parent + 2 * group
                real, imag = pair_up(
                    boxes[child, wedge].astype(jnp.float32),
                    boxes[child + 1, wedge].astype(jnp.float32),
                    left,
                )
                rows[wedge, parent * 16 : parent * 16 + 16, cut] = turned(real, imag, cosine[:, cut], sine[:, cut])
        result = product(rows[wedge], weights[wedge])
        for p in range(4):
            out[p, wedge] = joined(result[16 * p : 16 * p + 8], result[16 * p + 8 : 16 * p + 16], left)


def top_level(boxes, trig, weights):
    wedges = weights.shape[0]
    return pl.pallas_call(
        top_kernel,
        out_shape=jax.ShapeDtypeStruct((4, wedges, EXC, LANES), jnp.float32),
        scratch_shapes=[
            pltpu.VMEM((wedges, 64, FULL), jnp.bfloat16),
        ],
        compiler_params=pltpu.CompilerParams(vmem_limit_bytes=16 << 20),
        name="top_level",
    )(boxes, trig, weights)


def upward(
    leaf_density,
    phases_first,
    phases_switch,
    phases_top,
    transfer_first,
    transfer_switch,
    transfer_top,
    child_mid,
    child_top,
):
    def flat(weights):
        return weights.reshape(weights.shape[0], LANES, FULL)

    level_one, weights = first_level(
        leaf_density, phases_first.transpose(1, 0, 2), flat(transfer_first), flat(transfer_switch)
    )
    boxes = lax.axis_size("box")

    def moves(up, right):
        pairs = []
        for b in range(boxes):
            for y in range(Y_PAIR):
                for x in range(X_RING):
                    side = right if b % 2 == 0 else -right
                    to_y, to_x = (y + up) % Y_PAIR, (x + side) % X_RING
                    pairs.append(((b * Y_PAIR + y) * X_RING + x, (b * Y_PAIR + to_y) * X_RING + to_x))
        return pairs

    def shift(block, up, right):
        return lax.ppermute(block, ("box", "dir"), moves(up, right))

    other = shift(level_one, 1, 0)
    front = shift(level_one, 0, 1)
    back = shift(level_one, 0, -1)
    far = shift(front, 0, 1)
    other_front = shift(other, 0, 1)
    other_back = shift(back, 1, 0)
    other_far = shift(other_front, 0, 1)
    blocks = (level_one, other, front, back, far, other_front, other_back, other_far)
    switch_trig, top_trig = make_ready(phases_switch, phases_top.transpose(1, 0, 2), level_one)
    most, plan = switch_most(
        child_mid, child_top, blocks[:7], switch_trig, weights, transfer_top.shape[0]
    )
    send = switch_rest(plan, other_far, switch_trig, weights, most, boxes)
    received = lax.all_to_all(send, "box", 0, 0)
    return top_level(received, top_trig, flat(transfer_top))


def solution(mesh):
    placed = (
        P("box", "dir", None, None),
        P(None, "dir", None),
        P(None, "dir", None),
        P(None, ("box", "dir"), None),
        P("dir", None, None, None),
        P("dir", None, None, None),
        P(("box", "dir"), None, None, None),
        P("dir"),
        P(),
    )
    return jax.shard_map(
        upward,
        mesh=mesh,
        in_specs=placed,
        out_specs=P(None, ("box", "dir"), None, None),
        check_vma=False,
    )
```

```python
import functools

import jax
import jax.numpy as jnp
from jax import lax
from jax.experimental import pallas as pl
from jax.experimental.pallas import tpu as pltpu
from jax.sharding import PartitionSpec as P


HALF = 64
LANES = 128
EXC = 8
FULL = 8 * HALF
STEP_FIRST = 6
BATCH = 10
PLAN = 5
X_RING = 4
Y_PAIR = 2
OFFSETS = ((0, 0), (1, 0), (0, 1), (0, -1), (1, 1), (0, 2), (1, -1), (1, 2))
SOON = 5


def sin_cos(angle):
    turns = jnp.floor(angle * 0.6366197723675814 + 0.5)
    rest = angle - turns * 1.5703125
    rest = rest - turns * 4.837512969970703e-4
    rest = rest - turns * 7.549789948768648e-8
    square = rest * rest
    sine = rest + rest * square * (
        -1.6666654611e-1 + square * (8.3321608736e-3 - square * 1.9515295891e-4)
    )
    cosine = 1.0 - 0.5 * square + square * square * (
        4.166664568298827e-2 + square * (-1.388731625493765e-3 + square * 2.443315711809948e-5)
    )
    quarter = turns.astype(jnp.int32) & 3
    swap = (quarter & 1) == 1
    sine_abs = jnp.where(swap, cosine, sine)
    cosine_abs = jnp.where(swap, sine, cosine)
    sine_out = jnp.where(quarter >= 2, -sine_abs, sine_abs)
    cosine_out = jnp.where((quarter == 1) | (quarter == 2), -cosine_abs, cosine_abs)
    return sine_out, cosine_out


def left_lanes():
    return lax.broadcasted_iota(jnp.int32, (EXC, LANES), 1) < HALF


def flip(value):
    return pltpu.roll(value, HALF, 1)


def pair_up(first, second, left):
    real = jnp.where(left, first, flip(second))
    imag = jnp.where(left, flip(first), second)
    return real, imag


def turned(real, imag, cosine, sine):
    return jnp.concatenate(
        [cosine * real - sine * imag, sine * real + cosine * imag], axis=0
    ).astype(jnp.bfloat16)


def product(rows, weights):
    return lax.dot_general(
        rows, weights, (((1,), (1,)), ((), ())), preferred_element_type=jnp.float32
    )


def joined(real_rows, imag_rows, left):
    moved = flip(imag_rows)
    return real_rows + jnp.where(left, -moved, moved)


def in_hbm(value):
    return pltpu.with_memory_space_constraint(value, pltpu.HBM)


def fill_trig(trig, angle_of):
    for group in range(4):
        cut = slice(group * LANES, (group + 1) * LANES)
        angle = jnp.concatenate([angle_of(2 * group), angle_of(2 * group + 1)], axis=1)
        trig[0, :, cut], trig[1, :, cut] = sin_cos(angle)


def first_kernel(leaf_hbm, angles_hbm, weights_hbm, out, leaf, angles, weights, rows, trig, sems):
    left = left_lanes()
    wedges = leaf.shape[1]
    steps = wedges // STEP_FIRST

    def copies(step):
        part = pl.ds(step * STEP_FIRST, STEP_FIRST)
        return (
            pltpu.make_async_copy(leaf_hbm.at[:, part], leaf.at[:, part], sems.at[0, step]),
            pltpu.make_async_copy(weights_hbm.at[part], weights.at[part], sems.at[1, step]),
        )

    angle_copy = pltpu.make_async_copy(angles_hbm, angles, sems.at[0, steps])
    angle_copy.start()
    for step in range(steps):
        for copy in copies(step):
            copy.start()
    angle_copy.wait()
    fill_trig(trig, lambda child: angles[:, child, :])
    for wedge in range(wedges):
        if wedge % STEP_FIRST == 0:
            for copy in copies(wedge // STEP_FIRST):
                copy.wait()
        sine = trig[0, wedge : wedge + 1, :]
        cosine = trig[1, wedge : wedge + 1, :]
        place = wedge % 2
        for parent in range(8):
            for group in range(4):
                cut = slice(group * LANES, (group + 1) * LANES)
                child = 8 * parent + 2 * group
                real, imag = pair_up(
                    leaf[child, wedge].astype(jnp.float32),
                    leaf[child + 1, wedge].astype(jnp.float32),
                    left,
                )
                rows[place, parent * 16 : parent * 16 + 16, cut] = turned(real, imag, cosine[:, cut], sine[:, cut])
        result = product(rows[place], weights[wedge])
        pieces = [
            joined(result[16 * p : 16 * p + 8], result[16 * p + 8 : 16 * p + 16], left)
            for p in range(8)
        ]
        for group in range(4):
            real, imag = pair_up(pieces[2 * group], pieces[2 * group + 1], left)
            out[wedge, :, group * LANES : (group + 1) * LANES] = jnp.concatenate([real, imag], axis=0).astype(jnp.bfloat16)


def first_level(leaf, angles, weights):
    wedges = leaf.shape[1]
    hbm = pl.BlockSpec(memory_space=pltpu.HBM)
    return pl.pallas_call(
        first_kernel,
        out_shape=pltpu.VMEM((wedges, 16, FULL), jnp.bfloat16),
        in_specs=[hbm, hbm, hbm],
        out_specs=pl.BlockSpec(memory_space=pltpu.VMEM),
        scratch_shapes=[
            pltpu.VMEM(leaf.shape, jnp.bfloat16),
            pltpu.VMEM(angles.shape, jnp.float32),
            pltpu.VMEM(weights.shape, jnp.bfloat16),
            pltpu.VMEM((2, 128, FULL), jnp.bfloat16),
            pltpu.VMEM((2, wedges, FULL), jnp.float32),
            pltpu.SemaphoreType.DMA((2, wedges // STEP_FIRST + 1)),
        ],
        compiler_params=pltpu.CompilerParams(vmem_limit_bytes=12 << 20),
        name="first_level",
    )(in_hbm(leaf), in_hbm(angles), in_hbm(weights))


def ready_kernel(
    switch_hbm, top_hbm, weights_hbm, after,
    switch_trig, top_trig, weights,
    switch_angles, top_angles, sems,
):
    half = pl.ds(0, weights.shape[0] // 2)
    switch_copy = pltpu.make_async_copy(switch_hbm, switch_angles, sems.at[0])
    top_copy = pltpu.make_async_copy(top_hbm, top_angles, sems.at[1])
    weight_copy = pltpu.make_async_copy(weights_hbm.at[half], weights.at[half], sems.at[2])
    switch_copy.start()
    top_copy.start()
    weight_copy.start()
    switch_copy.wait()
    fill_trig(switch_trig, lambda child: switch_angles[child])
    top_copy.wait()
    fill_trig(top_trig, lambda child: top_angles[:, child, :])
    weight_copy.wait()


def make_ready(switch_angles, top_angles, weights, after):
    hbm = pl.BlockSpec(memory_space=pltpu.HBM)
    vmem = pl.BlockSpec(memory_space=pltpu.VMEM)
    return pl.pallas_call(
        ready_kernel,
        out_shape=(
            pltpu.VMEM((2, switch_angles.shape[1], FULL), jnp.float32),
            pltpu.VMEM((2, top_angles.shape[0], FULL), jnp.float32),
            pltpu.VMEM(weights.shape, jnp.bfloat16),
        ),
        in_specs=[hbm, hbm, hbm, pl.BlockSpec(memory_space=pl.ANY)],
        out_specs=(vmem, vmem, vmem),
        scratch_shapes=[
            pltpu.VMEM(switch_angles.shape, jnp.float32),
            pltpu.VMEM(top_angles.shape, jnp.float32),
            pltpu.SemaphoreType.DMA((3,)),
        ],
        compiler_params=pltpu.CompilerParams(vmem_limit_bytes=4 << 20),
        name="make_ready",
    )(in_hbm(switch_angles), in_hbm(top_angles), in_hbm(weights), after)


def weights_kernel(weights_hbm, after, partial, weights, sem):
    count = weights.shape[0]
    half = pl.ds(count // 2, count - count // 2)
    copy = pltpu.make_async_copy(weights_hbm.at[half], weights.at[half], sem)
    copy.start()
    copy.wait()


def make_weights(weights, after, partial):
    vmem = pl.BlockSpec(memory_space=pltpu.VMEM)
    return pl.pallas_call(
        weights_kernel,
        out_shape=pltpu.VMEM(weights.shape, jnp.bfloat16),
        in_specs=[pl.BlockSpec(memory_space=pltpu.HBM), pl.BlockSpec(memory_space=pl.ANY), vmem],
        out_specs=vmem,
        input_output_aliases={2: 0},
        scratch_shapes=[pltpu.SemaphoreType.DMA],
        compiler_params=pltpu.CompilerParams(vmem_limit_bytes=1 << 20),
        name="make_weights",
    )(in_hbm(weights), after, partial)


def lift_one(picked, trig, weights, wedge, left):
    rows = picked.astype(jnp.float32)
    sine = trig[0, pl.ds(wedge, 1), :]
    cosine = trig[1, pl.ds(wedge, 1), :]
    result = product(turned(rows[:8], rows[8:], cosine, sine), weights[wedge])
    return joined(result[:8], result[8:], left).astype(jnp.bfloat16)


def most_kernel(top_count, child_mid, child_top, *refs):
    blocks = refs[:SOON]
    trig, weights, level_two, plan, gathered = refs[SOON:]
    left = left_lanes()
    low = gathered.shape[0] // 8
    mid_count = level_two.shape[0]
    slots = plan.shape[0] - PLAN * mid_count
    share = lax.axis_index("dir").astype(jnp.int32)
    ahead = 1 - 2 * (lax.axis_index("box").astype(jnp.int32) & 1)
    row, column = share >> 2, share & (X_RING - 1)

    def first_wedge(up, right):
        return low * (((row + up) & 1) * X_RING + ((column - right * ahead) & (X_RING - 1)))

    for k in range(SOON):
        base = first_wedge(*OFFSETS[k])
        for i in range(low):
            gathered[base + i] = blocks[k][i]

    far, side, last = [first_wedge(*offset) for offset in OFFSETS[SOON:]]
    late = jnp.int32(0)
    final = jnp.int32(0)
    per_wedge = slots // mid_count
    for wedge in range(mid_count):
        source = child_mid[wedge]
        in_far = (source >= far) & (source < far + low)
        in_side = (source >= side) & (source < side + low)
        in_last = (source >= last) & (source < last + low)
        plan[slots + late] = wedge
        plan[slots + mid_count + late] = jnp.where(in_far, source - far, source - side + low)
        late = late + jnp.where(in_far | in_side, 1, 0)
        plan[slots + 2 * mid_count + final] = wedge
        plan[slots + 3 * mid_count + final] = source - last
        final = final + jnp.where(in_last, 1, 0)
        here = jnp.where(in_far | in_side | in_last, share * low, source)
        level_two[wedge] = lift_one(gathered[here], trig, weights, wedge, left)
        for slot in range(per_wedge * wedge, per_wedge * (wedge + 1)):
            top = (slot // top_count * 8 + share) * top_count + slot % top_count
            plan[slot] = child_top[top] - share * mid_count
    plan[slots + 4 * mid_count] = late
    plan[slots + 4 * mid_count + 1] = final


def switch_most(child_mid, child_top, blocks, trig, weights, top_count):
    mid_count = weights.shape[0]
    low = blocks[0].shape[0]
    smem = pl.BlockSpec(memory_space=pltpu.SMEM)
    vmem = pl.BlockSpec(memory_space=pltpu.VMEM)
    return pl.pallas_call(
        functools.partial(most_kernel, top_count),
        out_shape=(
            pltpu.VMEM((mid_count, EXC, LANES), jnp.bfloat16),
            jax.ShapeDtypeStruct((child_top.shape[0] // 8 + PLAN * mid_count,), jnp.int32),
        ),
        in_specs=[smem] * 2 + [vmem] * (SOON + 2),
        out_specs=(vmem, smem),
        scratch_shapes=[pltpu.VMEM((8 * low, 16, FULL), jnp.bfloat16)],
        compiler_params=pltpu.CompilerParams(vmem_limit_bytes=8 << 20),
        name="switch_most",
    )(child_mid, child_top, *blocks, trig, weights)


def lift_listed(plan, start, count, rows, trig, weights, level_two):
    left = left_lanes()
    mid_count = level_two.shape[0]

    def batch(step, carry):
        for i in range(BATCH):
            entry = start + jnp.minimum(step * BATCH + i, count - 1)
            wedge = plan[entry]
            level_two[wedge] = lift_one(rows[plan[mid_count + entry]], trig, weights, wedge, left)
        return carry

    lax.fori_loop(0, (count + BATCH - 1) // BATCH, batch, 0)


def late_kernel(plan, far, side, trig, weights, ready, level_two, gathered):
    mid_count, low = level_two.shape[0], far.shape[0]
    slots = plan.shape[0] - PLAN * mid_count
    for wedge in range(mid_count):
        level_two[wedge] = ready[wedge]
    for i in range(low):
        gathered[i] = far[i]
        gathered[low + i] = side[i]
    lift_listed(plan, slots, plan[slots + 4 * mid_count], gathered, trig, weights, level_two)


def switch_late(plan, far, side, trig, weights, ready):
    vmem = pl.BlockSpec(memory_space=pltpu.VMEM)
    return pl.pallas_call(
        late_kernel,
        out_shape=pltpu.VMEM(ready.shape, jnp.bfloat16),
        in_specs=[pl.BlockSpec(memory_space=pltpu.SMEM)] + [vmem] * 5,
        out_specs=vmem,
        scratch_shapes=[pltpu.VMEM((2 * far.shape[0], 16, FULL), jnp.bfloat16)],
        compiler_params=pltpu.CompilerParams(vmem_limit_bytes=4 << 20),
        name="switch_late",
    )(plan, far, side, trig, weights, ready)


def rest_kernel(plan, last, trig, weights, ready, out, level_two):
    mid_count = level_two.shape[0]
    slots = plan.shape[0] - PLAN * mid_count
    for wedge in range(mid_count):
        level_two[wedge] = ready[wedge]
    count = plan[slots + 4 * mid_count + 1]
    lift_listed(plan, slots + 2 * mid_count, count, last, trig, weights, level_two)
    top_count = out.shape[1]
    for slot in range(slots):
        out[slot // top_count, slot % top_count] = level_two[plan[slot]]


def switch_rest(plan, last, trig, weights, ready, devices):
    mid_count = weights.shape[0]
    slots = plan.shape[0] - PLAN * mid_count
    vmem = pl.BlockSpec(memory_space=pltpu.VMEM)
    return pl.pallas_call(
        rest_kernel,
        out_shape=jax.ShapeDtypeStruct((devices, slots // devices, EXC, LANES), jnp.bfloat16),
        in_specs=[pl.BlockSpec(memory_space=pltpu.SMEM)] + [vmem] * 4,
        scratch_shapes=[pltpu.VMEM(ready.shape, jnp.bfloat16)],
        compiler_params=pltpu.CompilerParams(vmem_limit_bytes=4 << 20),
        name="switch_rest",
    )(plan, last, trig, weights, ready)


def top_kernel(boxes, trig, weights, out, rows):
    left = left_lanes()
    wedges = weights.shape[0]
    for wedge in range(wedges):
        sine = trig[0, pl.ds(wedge, 1), :]
        cosine = trig[1, pl.ds(wedge, 1), :]
        for parent in range(4):
            for group in range(4):
                cut = slice(group * LANES, (group + 1) * LANES)
                child = 8 * parent + 2 * group
                real, imag = pair_up(
                    boxes[child, wedge].astype(jnp.float32),
                    boxes[child + 1, wedge].astype(jnp.float32),
                    left,
                )
                rows[wedge, parent * 16 : parent * 16 + 16, cut] = turned(real, imag, cosine[:, cut], sine[:, cut])
        result = product(rows[wedge], weights[wedge])
        for p in range(4):
            out[p, wedge] = joined(result[16 * p : 16 * p + 8], result[16 * p + 8 : 16 * p + 16], left)


def top_level(boxes, trig, weights):
    wedges = weights.shape[0]
    return pl.pallas_call(
        top_kernel,
        out_shape=jax.ShapeDtypeStruct((4, wedges, EXC, LANES), jnp.float32),
        scratch_shapes=[
            pltpu.VMEM((wedges, 64, FULL), jnp.bfloat16),
        ],
        compiler_params=pltpu.CompilerParams(vmem_limit_bytes=16 << 20),
        name="top_level",
    )(boxes, trig, weights)


def upward(
    leaf_density,
    phases_first,
    phases_switch,
    phases_top,
    transfer_first,
    transfer_switch,
    transfer_top,
    child_mid,
    child_top,
):
    def flat(weights):
        return weights.reshape(weights.shape[0], LANES, FULL)

    level_one = first_level(leaf_density, phases_first.transpose(1, 0, 2), flat(transfer_first))
    boxes = lax.axis_size("box")

    def moves(up, right):
        pairs = []
        for b in range(boxes):
            for y in range(Y_PAIR):
                for x in range(X_RING):
                    side = right if b % 2 == 0 else -right
                    to_y, to_x = (y + up) % Y_PAIR, (x + side) % X_RING
                    pairs.append(((b * Y_PAIR + y) * X_RING + x, (b * Y_PAIR + to_y) * X_RING + to_x))
        return pairs

    def shift(block, up, right):
        return lax.ppermute(block, ("box", "dir"), moves(up, right))

    other = shift(level_one, 1, 0)
    front = shift(level_one, 0, 1)
    back = shift(level_one, 0, -1)
    far = shift(front, 0, 1)
    other_front = shift(other, 0, 1)
    other_back = shift(back, 1, 0)
    other_far = shift(other_front, 0, 1)
    blocks = (level_one, other, front, back, other_front)
    switch_trig, top_trig, partial = make_ready(
        phases_switch, phases_top.transpose(1, 0, 2), flat(transfer_switch), level_one
    )
    weights = make_weights(flat(transfer_switch), back, partial)
    most, plan = switch_most(
        child_mid, child_top, blocks, switch_trig, weights, transfer_top.shape[0]
    )
    late = switch_late(plan, far, other_back, switch_trig, weights, most)
    send = switch_rest(plan, other_far, switch_trig, weights, late, boxes)
    received = lax.all_to_all(send, "box", 0, 0)
    return top_level(received, top_trig, flat(transfer_top))


def solution(mesh):
    placed = (
        P("box", "dir", None, None),
        P(None, "dir", None),
        P(None, "dir", None),
        P(None, ("box", "dir"), None),
        P("dir", None, None, None),
        P("dir", None, None, None),
        P(("box", "dir"), None, None, None),
        P("dir"),
        P(),
    )
    return jax.shard_map(
        upward,
        mesh=mesh,
        in_specs=placed,
        out_specs=P(None, ("box", "dir"), None, None),
        check_vma=False,
    )
```

```python
import functools

import jax
import jax.numpy as jnp
from jax import lax
from jax.experimental import pallas as pl
from jax.experimental.pallas import tpu as pltpu
from jax.sharding import PartitionSpec as P


HALF = 64
LANES = 128
EXC = 8
FULL = 8 * HALF
STEP_FIRST = 6
BATCH = 10
PLAN = 5
X_RING = 4
SOON = 5


def sin_cos(angle):
    turns = jnp.floor(angle * 0.6366197723675814 + 0.5)
    rest = angle - turns * 1.5703125
    rest = rest - turns * 4.837512969970703e-4
    rest = rest - turns * 7.549789948768648e-8
    square = rest * rest
    sine = rest + rest * square * (
        -1.6666654611e-1 + square * (8.3321608736e-3 - square * 1.9515295891e-4)
    )
    cosine = 1.0 - 0.5 * square + square * square * (
        4.166664568298827e-2 + square * (-1.388731625493765e-3 + square * 2.443315711809948e-5)
    )
    quarter = turns.astype(jnp.int32) & 3
    swap = (quarter & 1) == 1
    sine_abs = jnp.where(swap, cosine, sine)
    cosine_abs = jnp.where(swap, sine, cosine)
    sine_out = jnp.where(quarter >= 2, -sine_abs, sine_abs)
    cosine_out = jnp.where((quarter == 1) | (quarter == 2), -cosine_abs, cosine_abs)
    return sine_out, cosine_out


def left_lanes():
    return lax.broadcasted_iota(jnp.int32, (EXC, LANES), 1) < HALF


def flip(value):
    return pltpu.roll(value, HALF, 1)


def pair_up(first, second, left):
    real = jnp.where(left, first, flip(second))
    imag = jnp.where(left, flip(first), second)
    return real, imag


def turned(real, imag, cosine, sine):
    return jnp.concatenate(
        [cosine * real - sine * imag, sine * real + cosine * imag], axis=0
    ).astype(jnp.bfloat16)


def product(rows, weights):
    return lax.dot_general(
        rows, weights, (((1,), (1,)), ((), ())), preferred_element_type=jnp.float32
    )


def joined(real_rows, imag_rows, left):
    moved = flip(imag_rows)
    return real_rows + jnp.where(left, -moved, moved)


def in_hbm(value):
    return pltpu.with_memory_space_constraint(value, pltpu.HBM)


def fill_trig(trig, angle_of):
    for group in range(4):
        cut = slice(group * LANES, (group + 1) * LANES)
        angle = jnp.concatenate([angle_of(2 * group), angle_of(2 * group + 1)], axis=1)
        trig[0, :, cut], trig[1, :, cut] = sin_cos(angle)


def first_kernel(leaf_hbm, angles_hbm, weights_hbm, out, leaf, angles, weights, rows, trig, sems):
    left = left_lanes()
    wedges = leaf.shape[1]
    steps = wedges // STEP_FIRST

    def copies(step):
        part = pl.ds(step * STEP_FIRST, STEP_FIRST)
        return (
            pltpu.make_async_copy(leaf_hbm.at[:, part], leaf.at[:, part], sems.at[0, step]),
            pltpu.make_async_copy(weights_hbm.at[part], weights.at[part], sems.at[1, step]),
        )

    angle_copy = pltpu.make_async_copy(angles_hbm, angles, sems.at[0, steps])
    angle_copy.start()
    for step in range(steps):
        for copy in copies(step):
            copy.start()
    angle_copy.wait()
    fill_trig(trig, lambda child: angles[:, child, :])
    for wedge in range(wedges):
        if wedge % STEP_FIRST == 0:
            for copy in copies(wedge // STEP_FIRST):
                copy.wait()
        sine = trig[0, wedge : wedge + 1, :]
        cosine = trig[1, wedge : wedge + 1, :]
        place = wedge % 2
        for parent in range(8):
            for group in range(4):
                cut = slice(group * LANES, (group + 1) * LANES)
                child = 8 * parent + 2 * group
                real, imag = pair_up(
                    leaf[child, wedge].astype(jnp.float32),
                    leaf[child + 1, wedge].astype(jnp.float32),
                    left,
                )
                rows[place, parent * 16 : parent * 16 + 16, cut] = turned(real, imag, cosine[:, cut], sine[:, cut])
        result = product(rows[place], weights[wedge])
        pieces = [
            joined(result[16 * p : 16 * p + 8], result[16 * p + 8 : 16 * p + 16], left)
            for p in range(8)
        ]
        for group in range(4):
            real, imag = pair_up(pieces[2 * group], pieces[2 * group + 1], left)
            out[wedge, :, group * LANES : (group + 1) * LANES] = jnp.concatenate([real, imag], axis=0).astype(jnp.bfloat16)


def first_level(leaf, angles, weights):
    wedges = leaf.shape[1]
    hbm = pl.BlockSpec(memory_space=pltpu.HBM)
    return pl.pallas_call(
        first_kernel,
        out_shape=pltpu.VMEM((wedges, 16, FULL), jnp.bfloat16),
        in_specs=[hbm, hbm, hbm],
        out_specs=pl.BlockSpec(memory_space=pltpu.VMEM),
        scratch_shapes=[
            pltpu.VMEM(leaf.shape, jnp.bfloat16),
            pltpu.VMEM(angles.shape, jnp.float32),
            pltpu.VMEM(weights.shape, jnp.bfloat16),
            pltpu.VMEM((2, 128, FULL), jnp.bfloat16),
            pltpu.VMEM((2, wedges, FULL), jnp.float32),
            pltpu.SemaphoreType.DMA((2, wedges // STEP_FIRST + 1)),
        ],
        compiler_params=pltpu.CompilerParams(vmem_limit_bytes=12 << 20),
        name="first_level",
    )(in_hbm(leaf), in_hbm(angles), in_hbm(weights))


def ready_kernel(
    switch_hbm, top_hbm, weights_hbm, after,
    switch_trig, top_trig, weights,
    switch_angles, top_angles, sems,
):
    half = pl.ds(0, weights.shape[0] // 2)
    switch_copy = pltpu.make_async_copy(switch_hbm, switch_angles, sems.at[0])
    top_copy = pltpu.make_async_copy(top_hbm, top_angles, sems.at[1])
    weight_copy = pltpu.make_async_copy(weights_hbm.at[half], weights.at[half], sems.at[2])
    switch_copy.start()
    top_copy.start()
    weight_copy.start()
    switch_copy.wait()
    fill_trig(switch_trig, lambda child: switch_angles[child])
    top_copy.wait()
    fill_trig(top_trig, lambda child: top_angles[:, child, :])
    weight_copy.wait()


def make_ready(switch_angles, top_angles, weights, after):
    hbm = pl.BlockSpec(memory_space=pltpu.HBM)
    vmem = pl.BlockSpec(memory_space=pltpu.VMEM)
    return pl.pallas_call(
        ready_kernel,
        out_shape=(
            pltpu.VMEM((2, switch_angles.shape[1], FULL), jnp.float32),
            pltpu.VMEM((2, top_angles.shape[0], FULL), jnp.float32),
            pltpu.VMEM(weights.shape, jnp.bfloat16),
        ),
        in_specs=[hbm, hbm, hbm, pl.BlockSpec(memory_space=pl.ANY)],
        out_specs=(vmem, vmem, vmem),
        scratch_shapes=[
            pltpu.VMEM(switch_angles.shape, jnp.float32),
            pltpu.VMEM(top_angles.shape, jnp.float32),
            pltpu.SemaphoreType.DMA((3,)),
        ],
        compiler_params=pltpu.CompilerParams(vmem_limit_bytes=4 << 20),
        name="make_ready",
    )(in_hbm(switch_angles), in_hbm(top_angles), in_hbm(weights), after)


def weights_kernel(weights_hbm, after, partial, weights, sem):
    count = weights.shape[0]
    half = pl.ds(count // 2, count - count // 2)
    copy = pltpu.make_async_copy(weights_hbm.at[half], weights.at[half], sem)
    copy.start()
    copy.wait()


def make_weights(weights, after, partial):
    vmem = pl.BlockSpec(memory_space=pltpu.VMEM)
    return pl.pallas_call(
        weights_kernel,
        out_shape=pltpu.VMEM(weights.shape, jnp.bfloat16),
        in_specs=[pl.BlockSpec(memory_space=pltpu.HBM), pl.BlockSpec(memory_space=pl.ANY), vmem],
        out_specs=vmem,
        input_output_aliases={2: 0},
        scratch_shapes=[pltpu.SemaphoreType.DMA],
        compiler_params=pltpu.CompilerParams(vmem_limit_bytes=1 << 20),
        name="make_weights",
    )(in_hbm(weights), after, partial)


def lift_one(picked, trig, weights, wedge, left):
    rows = picked.astype(jnp.float32)
    sine = trig[0, pl.ds(wedge, 1), :]
    cosine = trig[1, pl.ds(wedge, 1), :]
    result = product(turned(rows[:8], rows[8:], cosine, sine), weights[wedge])
    return joined(result[:8], result[8:], left).astype(jnp.bfloat16)


def most_kernel(top_count, child_mid, child_top, *refs):
    blocks = refs[:SOON]
    trig, weights, level_two, plan, gathered = refs[SOON:]
    left = left_lanes()
    low = gathered.shape[0] // 8
    mid_count = level_two.shape[0]
    slots = plan.shape[0] - PLAN * mid_count
    share = lax.axis_index("dir").astype(jnp.int32)
    core = lax.axis_index("box").astype(jnp.int32) & 1
    front, back, opposite, row = 1 + 2 * core, 3 - 2 * core, 2, X_RING

    def first_wedge(turn):
        return low * (share ^ turn)

    soon = (0, row, front, back, row ^ back)
    for k in range(SOON):
        base = first_wedge(soon[k])
        for i in range(low):
            gathered[base + i] = blocks[k][i]

    far, side, last = [first_wedge(turn) for turn in (opposite, row ^ front, row ^ opposite)]
    late = jnp.int32(0)
    final = jnp.int32(0)
    per_wedge = slots // mid_count
    for wedge in range(mid_count):
        source = child_mid[wedge]
        in_far = (source >= far) & (source < far + low)
        in_side = (source >= side) & (source < side + low)
        in_last = (source >= last) & (source < last + low)
        plan[slots + late] = wedge
        plan[slots + mid_count + late] = jnp.where(in_far, source - far, source - side + low)
        late = late + jnp.where(in_far | in_side, 1, 0)
        plan[slots + 2 * mid_count + final] = wedge
        plan[slots + 3 * mid_count + final] = source - last
        final = final + jnp.where(in_last, 1, 0)
        here = jnp.where(in_far | in_side | in_last, share * low, source)
        level_two[wedge] = lift_one(gathered[here], trig, weights, wedge, left)
        for slot in range(per_wedge * wedge, per_wedge * (wedge + 1)):
            top = (slot // top_count * 8 + share) * top_count + slot % top_count
            plan[slot] = child_top[top] - share * mid_count
    plan[slots + 4 * mid_count] = late
    plan[slots + 4 * mid_count + 1] = final


def switch_most(child_mid, child_top, blocks, trig, weights, top_count):
    mid_count = weights.shape[0]
    low = blocks[0].shape[0]
    smem = pl.BlockSpec(memory_space=pltpu.SMEM)
    vmem = pl.BlockSpec(memory_space=pltpu.VMEM)
    return pl.pallas_call(
        functools.partial(most_kernel, top_count),
        out_shape=(
            pltpu.VMEM((mid_count, EXC, LANES), jnp.bfloat16),
            jax.ShapeDtypeStruct((child_top.shape[0] // 8 + PLAN * mid_count,), jnp.int32),
        ),
        in_specs=[smem] * 2 + [vmem] * (SOON + 2),
        out_specs=(vmem, smem),
        scratch_shapes=[pltpu.VMEM((8 * low, 16, FULL), jnp.bfloat16)],
        compiler_params=pltpu.CompilerParams(vmem_limit_bytes=8 << 20),
        name="switch_most",
    )(child_mid, child_top, *blocks, trig, weights)


def lift_listed(plan, start, count, rows, trig, weights, level_two):
    left = left_lanes()
    mid_count = level_two.shape[0]

    def batch(step, carry):
        for i in range(BATCH):
            entry = start + jnp.minimum(step * BATCH + i, count - 1)
            wedge = plan[entry]
            level_two[wedge] = lift_one(rows[plan[mid_count + entry]], trig, weights, wedge, left)
        return carry

    lax.fori_loop(0, (count + BATCH - 1) // BATCH, batch, 0)


def late_kernel(plan, far, side, trig, weights, ready, level_two, gathered):
    mid_count, low = level_two.shape[0], far.shape[0]
    slots = plan.shape[0] - PLAN * mid_count
    for wedge in range(mid_count):
        level_two[wedge] = ready[wedge]
    for i in range(low):
        gathered[i] = far[i]
        gathered[low + i] = side[i]
    lift_listed(plan, slots, plan[slots + 4 * mid_count], gathered, trig, weights, level_two)


def switch_late(plan, far, side, trig, weights, ready):
    vmem = pl.BlockSpec(memory_space=pltpu.VMEM)
    return pl.pallas_call(
        late_kernel,
        out_shape=pltpu.VMEM(ready.shape, jnp.bfloat16),
        in_specs=[pl.BlockSpec(memory_space=pltpu.SMEM)] + [vmem] * 5,
        out_specs=vmem,
        scratch_shapes=[pltpu.VMEM((2 * far.shape[0], 16, FULL), jnp.bfloat16)],
        compiler_params=pltpu.CompilerParams(vmem_limit_bytes=4 << 20),
        name="switch_late",
    )(plan, far, side, trig, weights, ready)


def rest_kernel(plan, last, trig, weights, ready, out, level_two):
    mid_count = level_two.shape[0]
    slots = plan.shape[0] - PLAN * mid_count
    for wedge in range(mid_count):
        level_two[wedge] = ready[wedge]
    count = plan[slots + 4 * mid_count + 1]
    lift_listed(plan, slots + 2 * mid_count, count, last, trig, weights, level_two)
    top_count = out.shape[1]
    for slot in range(slots):
        out[slot // top_count, slot % top_count] = level_two[plan[slot]]


def switch_rest(plan, last, trig, weights, ready, devices):
    mid_count = weights.shape[0]
    slots = plan.shape[0] - PLAN * mid_count
    vmem = pl.BlockSpec(memory_space=pltpu.VMEM)
    return pl.pallas_call(
        rest_kernel,
        out_shape=jax.ShapeDtypeStruct((devices, slots // devices, EXC, LANES), jnp.bfloat16),
        in_specs=[pl.BlockSpec(memory_space=pltpu.SMEM)] + [vmem] * 4,
        scratch_shapes=[pltpu.VMEM(ready.shape, jnp.bfloat16)],
        compiler_params=pltpu.CompilerParams(vmem_limit_bytes=4 << 20),
        name="switch_rest",
    )(plan, last, trig, weights, ready)


def top_kernel(boxes, trig, weights, out, rows):
    left = left_lanes()
    wedges = weights.shape[0]
    for wedge in range(wedges):
        sine = trig[0, pl.ds(wedge, 1), :]
        cosine = trig[1, pl.ds(wedge, 1), :]
        for parent in range(4):
            for group in range(4):
                cut = slice(group * LANES, (group + 1) * LANES)
                child = 8 * parent + 2 * group
                real, imag = pair_up(
                    boxes[child, wedge].astype(jnp.float32),
                    boxes[child + 1, wedge].astype(jnp.float32),
                    left,
                )
                rows[wedge, parent * 16 : parent * 16 + 16, cut] = turned(real, imag, cosine[:, cut], sine[:, cut])
        result = product(rows[wedge], weights[wedge])
        for p in range(4):
            out[p, wedge] = joined(result[16 * p : 16 * p + 8], result[16 * p + 8 : 16 * p + 16], left)


def top_level(boxes, trig, weights):
    wedges = weights.shape[0]
    return pl.pallas_call(
        top_kernel,
        out_shape=jax.ShapeDtypeStruct((4, wedges, EXC, LANES), jnp.float32),
        scratch_shapes=[
            pltpu.VMEM((wedges, 64, FULL), jnp.bfloat16),
        ],
        compiler_params=pltpu.CompilerParams(vmem_limit_bytes=16 << 20),
        name="top_level",
    )(boxes, trig, weights)


def upward(
    leaf_density,
    phases_first,
    phases_switch,
    phases_top,
    transfer_first,
    transfer_switch,
    transfer_top,
    child_mid,
    child_top,
):
    def flat(weights):
        return weights.reshape(weights.shape[0], LANES, FULL)

    level_one = first_level(leaf_density, phases_first.transpose(1, 0, 2), flat(transfer_first))
    boxes = lax.axis_size("box")

    group = lax.axis_size("dir")

    def shift(block, *turns):
        pairs = [
            (b * group + d, b * group + (d ^ turns[b % 2]))
            for b in range(boxes)
            for d in range(group)
        ]
        return lax.ppermute(block, ("box", "dir"), pairs)

    row, front_turns, back_turns = (X_RING, X_RING), (1, 3), (3, 1)
    other = shift(level_one, *row)
    back = shift(level_one, *back_turns)
    front = shift(level_one, *front_turns)
    other_back = shift(other, *back_turns)
    far = shift(back, *front_turns)
    other_front = shift(front, *row)
    other_far = shift(other_back, *front_turns)
    blocks = (level_one, other, front, back, other_back)
    switch_trig, top_trig, partial = make_ready(
        phases_switch, phases_top.transpose(1, 0, 2), flat(transfer_switch), level_one
    )
    weights = make_weights(flat(transfer_switch), front, partial)
    most, plan = switch_most(
        child_mid, child_top, blocks, switch_trig, weights, transfer_top.shape[0]
    )
    late = switch_late(plan, far, other_front, switch_trig, weights, most)
    send = switch_rest(plan, other_far, switch_trig, weights, late, boxes)
    received = lax.all_to_all(send, "box", 0, 0)
    return top_level(received, top_trig, flat(transfer_top))


def solution(mesh):
    placed = (
        P("box", "dir", None, None),
        P(None, "dir", None),
        P(None, "dir", None),
        P(None, ("box", "dir"), None),
        P("dir", None, None, None),
        P("dir", None, None, None),
        P(("box", "dir"), None, None, None),
        P("dir"),
        P(),
    )
    return jax.shard_map(
        upward,
        mesh=mesh,
        in_specs=placed,
        out_specs=P(None, ("box", "dir"), None, None),
        check_vma=False,
    )
```
